256 devices in a mesh: expert: 64 (over y, z, core), hidden: 4 (over x).
Axes of the slice: x: 4, y: 4, z: 8, core: 2. Of those that a mesh axis runs over, the one named last changes fastest.
Arguments:
- tokens: bfloat16 [8192, 4096], P('expert', 'hidden'), may hold values from -6 to 6
- routes: int32 [8192, 8], P('expert'), may hold values from 0 to 63, all different within a row; in each aligned block of 128 rows (0 to 127, 128 to 255, ...) at most 24 rows name the same one
- route_gates: float32 [8192, 8], P('expert'), may hold values from 0.03 to 0.3
- loss_weights: float32 [8192], P('expert'), may hold values from 0.25 to 4
- damping: float32 [1], replicated, may hold values from 1 to 16
- w_gate: bfloat16 [64, 4096, 768], P('expert', None, 'hidden'), may hold values from -0.09375 to 0.09375
- w_up: bfloat16 [64, 4096, 768], P('expert', None, 'hidden'), may hold values from -0.09375 to 0.09375
- direction: bfloat16 [64, 768, 4096], P('expert', 'hidden'), may hold values from -6 to 6
- residual: bfloat16 [64, 768, 4096], P('expert', 'hidden'), may hold values from -6 to 6
Outputs:
- solution_step: bfloat16 [64, 768, 4096], P('expert', 'hidden')
- new_residual: bfloat16 [64, 768, 4096], P('expert', 'hidden')
- new_direction: bfloat16 [64, 768, 4096], P('expert', 'hidden')
The draws below stay inside these ranges and needn't reach their ends.
Inputs may be any that keep to these rules, and one draw needn't show every extreme that they name: `routes`: each token names 8 different experts. Among the tokens of one index of expert (aligned blocks of 128 rows) no expert is named more than 24 times, and in every draw some block names some expert exactly 24 times.
All inputs are finite; a program needn't handle non-finite values.
Results may differ from the reference program's by a relative error of at most 0.011.
Values may be sent and summed in bfloat16 or wider, within the bound.
A program may use at most 128 MiB of HBM per device.

```python
import math
import jax
import jax.numpy as jnp
import numpy as np
from jax import lax

D = 4096
FF = 768
TOPK = 8
TOK_DEV = 128
EXPERTS = 64
TOKENS = 8192
CAP = 24
SLOTS = 1536


def block_levels(key, shape, cuts, low, top_value):
    gain = 1.0
    for dim, shards_of in cuts:
        heights = jax.random.uniform(jax.random.fold_in(jax.random.fold_in(key, 6), dim), (shards_of,), jnp.float32, low / len(cuts), top_value / len(cuts))
        gain = gain * jnp.repeat(jnp.exp(heights), shape[dim] // shards_of).reshape((-1,) + (1,) * (len(shape) - 1 - dim))
    return gain


def routed_block(stream_key, own, number, rows, count, top, most, lean):
    sequence = jax.random.permutation(stream_key, count)
    crowded, usual = load_shares(count, rows * top, most, lean, True), load_shares(count, rows * top, most, lean, False)
    places = jnp.arange(count)

    def named(lengths, offset_by):
        used = int((lengths > 0).sum())
        fixed = max(1, used // 4)
        passed = fixed + (places - fixed + offset_by * (used - fixed)) % max(1, count - fixed)
        return jnp.zeros((count,), jnp.int32).at[sequence[jnp.where(places < fixed, places, passed)]].set(jnp.asarray(lengths, jnp.int32))

    lengths = jnp.where(number % 4 == 0, named(crowded, number // 4), named(usual, number - number // 4 - 1))
    mixed = jax.random.permutation(jax.random.fold_in(own, 3), count)
    giver, taker = mixed[0:count // 2 * 2:2], mixed[1:count // 2 * 2:2]
    slack = jnp.minimum(lengths[giver] - 1, most - lengths[taker]) // 2
    slack = jnp.where((giver == sequence[0]) | (taker == sequence[0]) | (lengths[taker] == 0), 0, jnp.maximum(slack, 0))
    passed = jax.random.randint(jax.random.fold_in(own, 4), (count // 2,), 0, 1 << 20) % (slack + 1)
    lengths = lengths.at[giver].add(-passed).at[taker].add(passed)
    members = jnp.searchsorted(jnp.cumsum(lengths), jnp.arange(rows * top), side="right").astype(jnp.int32)
    listing = members.reshape(top, rows).T
    listing = listing[jax.random.permutation(jax.random.fold_in(own, 1), rows)]
    offset_by = jax.random.randint(jax.random.fold_in(own, 2), (rows, 1), 0, top)
    return jnp.take_along_axis(listing, (jnp.arange(top)[None, :] + offset_by) % top, axis=1)


def load_shares(count, total, most, lean, full):
    weights = [(1 << 20) // math.isqrt(standing ** lean) + 1 for standing in range(1, count + 1)]
    largest = most if full else min(most, max(-(-total // count), total * weights[0] // sum(weights)))
    least = 1 if total - largest >= count - 1 else 0
    counts, surplus = [largest] + [least] * (count - 1), total - largest - least * (count - 1)
    while surplus > 0:
        free = [i for i in range(1, count) if counts[i] < largest] or [i for i in range(1, count) if counts[i] < most]
        whole, left = sum([weights[i] for i in free]), surplus
        for i in free:
            addition = min(most - counts[i], max(1, left * weights[i] // whole), surplus)
            counts[i] = counts[i] + addition
            surplus = surplus - addition
    return np.array(counts)


def normal_values(key, extent, width, most, cuts=(), kind=jnp.bfloat16):
    gain = block_levels(key, extent, cuts, -0.22, 0.18) if cuts else 1.0
    entries = jax.random.normal(key, extent, jnp.float32) * width * gain
    return jnp.minimum(jnp.maximum(entries, -most), most).astype(kind)


def setup_inputs(seed: int = 0) -> dict:
    seeds = jax.random.split(jax.random.key(seed), 10)
    tokens = normal_values(seeds[0], (TOKENS, D), 1.0, 6.0, ((0, 64), (1, 4)))
    routes_keys = jax.random.split(jax.random.fold_in(seeds[1], 1), TOKENS // TOK_DEV)
    routes_turns = jax.random.permutation(jax.random.fold_in(seeds[1], 3), TOKENS // TOK_DEV)
    routes = jax.vmap(lambda own, number: routed_block(jax.random.fold_in(seeds[1], 2), own, number, TOK_DEV, EXPERTS, TOPK, CAP, 2))(routes_keys, routes_turns).reshape((TOKENS, TOPK))
    route_gates = jnp.clip(jnp.exp(math.log(0.3) - 2.3025852 * jax.random.uniform(seeds[2], (TOKENS, TOPK), jnp.float32) ** block_levels(seeds[2], (TOKENS, TOPK), ((0, 64),), -0.2, 0.2)), 0.03, 0.3)
    loss_weights = jnp.clip(jnp.exp(math.log(4.0) - 2.7725887 * jax.random.uniform(seeds[3], (TOKENS,), jnp.float32) ** block_levels(seeds[3], (TOKENS,), ((0, 64),), -0.2, 0.2)), 0.25, 4.0)
    damping = jnp.clip(jnp.exp(jax.random.uniform(seeds[4], (1,), jnp.float32, math.log(1.0), math.log(16.0))), 1.0, 16.0)
    w_gate = normal_values(seeds[5], (EXPERTS, D, FF), D ** -0.5, 0.09375, ((0, 64), (2, 4)))
    w_up = normal_values(seeds[6], (EXPERTS, D, FF), D ** -0.5, 0.09375, ((0, 64), (2, 4)))
    direction = normal_values(seeds[7], (EXPERTS, FF, D), 1.0, 6.0, ((0, 64), (1, 4)))
    residual = normal_values(seeds[8], (EXPERTS, FF, D), 1.0, 6.0, ((0, 64), (1, 4)))
    return dict(tokens=tokens, routes=routes, route_gates=route_gates, loss_weights=loss_weights, damping=damping, w_gate=w_gate, w_up=w_up, direction=direction, residual=residual)


def reference(tokens, routes, route_gates, loss_weights, damping, w_gate, w_up, direction, residual):
    flat_routes = routes.reshape(-1)
    flat_gates = route_gates.reshape(-1)
    total = TOKENS * TOPK

    def expert_rows(expert_id):
        found = jnp.nonzero(flat_routes == expert_id, size=SLOTS, fill_value=total)[0].astype(jnp.int32)
        filled = found < total
        safe = jnp.minimum(found, total - 1).astype(jnp.int32)
        return safe, filled

    def forward(combined, expert_id):
        safe, filled = expert_rows(expert_id)
        owner = safe // TOPK
        rows = jnp.where(filled[:, None], tokens[owner], jnp.zeros((), jnp.bfloat16))
        pre_gate = jnp.dot(rows, w_gate[expert_id], preferred_element_type=jnp.float32)
        pre_up = jnp.dot(rows, w_up[expert_id], preferred_element_type=jnp.float32)
        hidden = (jax.nn.silu(pre_gate) * pre_up).astype(jnp.bfloat16)
        tangent = jnp.dot(hidden, direction[expert_id], preferred_element_type=jnp.float32).astype(jnp.bfloat16)
        gates = jnp.where(filled, flat_gates[safe], jnp.zeros((), jnp.float32))
        combined = combined.at[owner].add(gates[:, None] * tangent.astype(jnp.float32))
        return combined, hidden

    combined, hidden_all = lax.scan(forward, jnp.zeros((TOKENS, D), jnp.float32), jnp.arange(EXPERTS, dtype=jnp.int32))
    scaled = combined * loss_weights[:, None]

    def curvature_of(inputs):
        expert_id, hidden = inputs
        safe, filled = expert_rows(expert_id)
        owner = safe // TOPK
        gates = jnp.where(filled, flat_gates[safe], jnp.zeros((), jnp.float32))
        cotangent = (gates[:, None] * scaled[owner]).astype(jnp.bfloat16)
        curvature = jnp.dot(hidden.T, cotangent, preferred_element_type=jnp.float32)
        search = direction[expert_id].astype(jnp.float32)
        resid = residual[expert_id].astype(jnp.float32)
        image = search + curvature / damping[0]
        return image, jnp.sum(search * image), jnp.sum(resid * resid)

    image_all, pq_parts, rr_parts = lax.map(curvature_of, (jnp.arange(EXPERTS, dtype=jnp.int32), hidden_all))
    pq_total = jnp.sum(pq_parts)
    rr_total = jnp.sum(rr_parts)
    alpha = rr_total / pq_total
    search_all = direction.astype(jnp.float32)
    updated = residual.astype(jnp.float32) - alpha * image_all
    rr_new = jnp.sum(updated * updated)
    beta = rr_new / rr_total
    solution_step = (alpha * search_all).astype(jnp.bfloat16)
    new_residual = updated.astype(jnp.bfloat16)
    new_direction = (updated + beta * search_all).astype(jnp.bfloat16)
    return solution_step, new_residual, new_direction
```

```python
import jax
import jax.numpy as jnp
from jax import lax
from jax.experimental import pallas as pl
from jax.experimental.pallas import tpu as pltpu
from jax.sharding import PartitionSpec as P

MESH = pl.DeviceIdType.MESH
BF = jnp.bfloat16
F32 = jnp.float32
NY, NZ, NC, NX = 4, 8, 2, 4
NQ = NY * NC
CAP = 24
TOK = 128
CH = 256
NK = 4
VMEM = pl.BlockSpec(memory_space=pltpu.VMEM)
ANY = pl.BlockSpec(memory_space=pl.ANY)


class Place:
    def __init__(self):
        self.e = lax.axis_index("expert")
        self.x = lax.axis_index("hidden")
        self.y = self.e // (NZ * NC)
        self.z = (self.e // NC) % NZ
        self.c = self.e % NC

    def expert(self, dy, dz, dc):
        return (
            ((self.y + dy) % NY) * (NZ * NC)
            + ((self.z + dz) % NZ) * NC
            + (self.c + dc) % NC
        )

    def q(self, q):
        return (self.expert(q // NC, 0, q % NC), self.x)

    def dz(self, d):
        return (self.expert(0, d, 0), self.x)

    def dx(self, d):
        return (self.e, self.xi(d))

    def xi(self, d):
        return (self.x + d) % NX


def inverse(q):
    return ((NY - q // NC) % NY) * NC + q % NC


def enter(peers):
    barrier = pltpu.get_barrier_semaphore()
    for peer in peers:
        pl.semaphore_signal(barrier, inc=1, device_id=peer, device_id_type=MESH)
    pl.semaphore_wait(barrier, len(peers))


def send(src, dst, ssem, rsem, peer):
    pltpu.make_async_remote_copy(
        src_ref=src, dst_ref=dst, send_sem=ssem, recv_sem=rsem, device_id=peer, device_id_type=MESH
    ).start()


def wait_bytes(ref, sem):
    pltpu.make_async_copy(ref, ref, sem).wait()


def pair_blocks(pi):
    return (0, 4) if pi == 3 else (pi + 1, NZ - 1 - pi)


def slot_matrix(tab_ref, pi, weighted):
    r0, r1 = pair_blocks(pi)
    slot = lax.broadcasted_iota(jnp.int32, (CAP, TOK), 0).astype(F32)
    zero = jnp.zeros((CAP, TOK), F32)
    rows = []
    for q in range(NQ):
        parts = []
        for r in (r0, r1):
            hit = tab_ref[r, q : q + 1, :] == slot
            value = tab_ref[r, NQ + q : NQ + q + 1, :] if weighted else jnp.ones((1, TOK), F32)
            parts.append(jnp.where(hit, value, 0.0))
        rows.append(jnp.concatenate([parts[0], zero], axis=1))
        rows.append(jnp.concatenate([zero, parts[1]], axis=1))
    return jnp.concatenate(rows, axis=0)


def lanes(k):
    return pl.ds(k * CH, CH)


def sign(k):
    return 1 if k % 2 == 0 else -1


def rel(r):
    return r % NZ


def tokens_kernel(
    routes_ref, gates_ref, tok_ref, wg_ref, wu_ref, dir_ref,
    x_ref, w_ref, dirc_ref, tab_ref,
    own_tab, slots, zb, ysend, wgv, wuv, wsend, wrecv,
    tab_ssem, tab_rsem, z_ssem, z_rsem, y_ssem, y_rsem, d_ssem, d_rsem, w_ssem, w_rsem, loc,
):
    at = Place()
    wg_load = pltpu.make_async_copy(wg_ref, wgv, loc.at[0])
    wu_load = pltpu.make_async_copy(wu_ref, wuv, loc.at[1])
    wg_load.start()
    wu_load.start()
    depth = dir_ref.shape[1] // NX
    ff = dir_ref.shape[0]
    own_dir = pltpu.make_async_copy(
        dir_ref.at[:, pl.ds(pl.multiple_of(at.x * depth, depth), depth)], dirc_ref.at[at.x], loc.at[2]
    )
    own_dir.start()

    row = lax.broadcasted_iota(jnp.int32, (NZ * NQ, TOK), 0)
    ids = (
        ((at.y + ((row >> 1) & 3)) & (NY - 1)) * (NZ * NC)
        + ((at.z + (row >> 3)) & (NZ - 1)) * NC
        + ((at.c + row) & 1)
    )
    named = jnp.zeros((NZ * NQ, TOK), F32)
    gate = jnp.zeros((NZ * NQ, TOK), F32)
    for j in range(routes_ref.shape[0]):
        same = routes_ref[j : j + 1, :] == ids
        named = named + jnp.where(same, 1.0, 0.0)
        gate = gate + jnp.where(same, gates_ref[j : j + 1, :], 0.0)
    before = (
        lax.broadcasted_iota(jnp.int32, (TOK, TOK), 0) < lax.broadcasted_iota(jnp.int32, (TOK, TOK), 1)
    )
    place = jnp.dot(
        named.astype(BF), jnp.where(before, 1.0, 0.0).astype(BF), preferred_element_type=F32
    )
    place = jnp.where(named > 0.0, place, -1.0)
    for r in range(NZ):
        own_tab[r, 0:NQ, :] = place[r * NQ : (r + 1) * NQ]
        own_tab[r, NQ : 2 * NQ, :] = gate[r * NQ : (r + 1) * NQ]
    tab_ref[0] = own_tab[0]

    enter(
        [at.q(q) for q in range(1, NQ)] + [at.dz(d) for d in range(1, NZ)] + [at.dx(d) for d in range(1, NX)]
    )
    for r in (1, 7, 2, 6, 3, 5, 4):
        send(own_tab.at[r], tab_ref.at[rel(-r)], tab_ssem, tab_rsem.at[rel(-r)], at.dz(r))
    for k in range(NK):
        for d in (1, -1):
            send(
                tok_ref.at[:, lanes(k)], zb.at[k, rel(-d)], z_ssem, z_rsem.at[k, rel(-d)], at.dz(d)
            )
    for d in (2, 1, 3):
        send(
            dir_ref.at[:, pl.ds(pl.multiple_of(at.xi(d) * depth, depth), depth)],
            dirc_ref.at[at.x], d_ssem, d_rsem, at.dx(d),
        )

    wg_load.wait()
    wu_load.wait()
    step = 64
    for d in (2, 1, 3, 0):
        base = at.xi(d) * depth

        def join(i, _, d=d, base=base):
            rows = pl.ds(pl.multiple_of(base + i * step, step), step)
            both = jnp.concatenate([wgv[rows, :], wuv[rows, :]], axis=1)
            out_rows = pl.ds(pl.multiple_of(i * step, step), step)
            if d == 0:
                wrecv[at.x, out_rows, :] = both
            else:
                wsend[d, out_rows, :] = both
            return 0

        lax.fori_loop(0, depth // step, join, 0)
        if d:
            send(wsend.at[d], wrecv.at[at.x], w_ssem, w_rsem, at.dx(d))

    for s in range(1, 5):
        pi = s - 1
        for r in pair_blocks(pi):
            if r:
                wait_bytes(tab_ref.at[r], tab_rsem.at[r])
        slots[pi] = slot_matrix(tab_ref, pi, False).astype(BF)
        for k in range(NK):
            d = sign(k)
            wait_bytes(zb.at[k, rel(-d * s)], z_rsem.at[k, rel(-d * s)])
            if s < 4:
                wait_bytes(zb.at[k, rel(d * s)], z_rsem.at[k, rel(d * s)])
                send(
                    zb.at[k, rel(-d * s)], zb.at[k, rel(-d * (s + 1))],
                    z_ssem, z_rsem.at[k, rel(-d * (s + 1))], at.dz(d),
                )
            if s < 3:
                send(
                    zb.at[k, rel(d * s)], zb.at[k, rel(d * (s + 1))],
                    z_ssem, z_rsem.at[k, rel(d * (s + 1))], at.dz(-d),
                )
            r0, r1 = pair_blocks(pi)
            first = tok_ref[:, lanes(k)] if r0 == 0 else zb[k, r0]
            block = jnp.concatenate([first, zb[k, r1]], axis=0)
            picked = jnp.dot(slots[pi], block, preferred_element_type=F32).astype(BF)
            rows = pl.ds(pi * 2 * CAP, 2 * CAP)
            x_ref[0, rows, lanes(k)] = picked[0 : 2 * CAP]
            for q in range(1, NQ):
                ysend[q, rows, lanes(k)] = picked[q * 2 * CAP : (q + 1) * 2 * CAP]
            for q in range(1, NQ):
                send(
                    ysend.at[q, rows, lanes(k)], x_ref.at[inverse(q), rows, lanes(k)],
                    y_ssem, y_rsem, at.q(q),
                )

    own_dir.wait()
    wait_bytes(wsend.at[pl.ds(1, 3)], w_rsem)

    def split(i, _):
        rows = pl.ds(pl.multiple_of(i * step, step), step)
        parts = [wrecv[j, rows, :] for j in range(NX)]
        w_ref[rows, :] = jnp.concatenate(
            [p[:, :ff] for p in parts] + [p[:, ff:] for p in parts], axis=1
        )
        return 0

    lax.fori_loop(0, depth // step, split, 0)
    wait_bytes(dirc_ref.at[pl.ds(1, 3)], d_rsem)
    wait_bytes(x_ref.at[pl.ds(1, NQ - 1)], y_rsem)
    wait_bytes(own_tab.at[pl.ds(1, NZ - 1)], tab_ssem)
    wait_bytes(zb.at[:, pl.ds(1, NZ - 1)], z_ssem)
    wait_bytes(x_ref.at[pl.ds(1, NQ - 1)], y_ssem)
    wait_bytes(dirc_ref.at[pl.ds(1, 3)], d_ssem)
    wait_bytes(wsend.at[pl.ds(1, 3)], w_ssem)


def hidden_kernel(
    p_ref, h_ref, far, acc, accin, near,
    f_ssem, f_rsem, a_ssem, a_rsem, n_ssem, n_rsem, h_ssem, h_rsem,
):
    at = Place()
    subs = far.shape[0]
    rows_of = far.shape[1]
    ff = h_ref.shape[2]
    step = 16
    enter([at.dx(1), at.dx(-1)])

    def rows(u):
        return pl.ds(u * rows_of, rows_of)

    for u in range(subs):
        d = sign(u)
        send(p_ref.at[at.xi(2), rows(u)], far.at[u], f_ssem, f_rsem.at[u], at.dx(-d))
        send(p_ref.at[at.xi(d), rows(u)], near.at[u], n_ssem, n_rsem.at[u], at.dx(d))
    for u in range(subs):
        d = sign(u)
        wait_bytes(far.at[u], f_rsem.at[u])

        def add(i, _, u=u, d=d):
            sub = pl.ds(pl.multiple_of(i * step, step), step)
            mine = p_ref[at.xi(-d), pl.ds(pl.multiple_of(u * rows_of + i * step, step), step), :]
            acc[u, sub, :] = (far[u, sub, :].astype(F32) + mine.astype(F32)).astype(BF)
            return 0

        lax.fori_loop(0, rows_of // step, add, 0)
        send(acc.at[u], accin.at[u], a_ssem, a_rsem.at[u], at.dx(-d))
    for u in range(subs):
        d = sign(u)
        wait_bytes(near.at[u], n_rsem.at[u])
        wait_bytes(accin.at[u], a_rsem.at[u])

        def act(i, _, u=u):
            sub = pl.ds(pl.multiple_of(i * step, step), step)
            whole = pl.ds(pl.multiple_of(u * rows_of + i * step, step), step)

            def total(cols):
                return (
                    p_ref[at.x, whole, cols].astype(F32)
                    + accin[u, sub, cols].astype(F32)
                    + near[u, sub, cols].astype(F32)
                )

            v = total(pl.ds(0, ff))
            h_ref[at.x, whole, :] = (v / (1.0 + jnp.exp(-v)) * total(pl.ds(ff, ff))).astype(BF)
            return 0

        lax.fori_loop(0, rows_of // step, act, 0)
        for t in (d, -d):
            send(
                h_ref.at[at.x, rows(u)], h_ref.at[at.x, rows(u)],
                h_ssem, h_rsem.at[u, 0 if t == d else 1], at.dx(t),
            )
    for u in range(subs):
        d = sign(u)
        wait_bytes(h_ref.at[at.xi(-d), rows(u)], h_rsem.at[u, 0])
        send(
            h_ref.at[at.xi(-d), rows(u)], h_ref.at[at.xi(-d), rows(u)],
            h_ssem, h_rsem.at[u, 2], at.dx(d),
        )
    for u in range(subs):
        d = sign(u)
        wait_bytes(h_ref.at[at.xi(d), rows(u)], h_rsem.at[u, 1])
        wait_bytes(h_ref.at[at.xi(2), rows(u)], h_rsem.at[u, 2])
    wait_bytes(far, f_ssem)
    wait_bytes(near, n_ssem)
    wait_bytes(acc, a_ssem)
    wait_bytes(h_ref.at[pl.ds(0, 3)], h_ssem)


def cotangent_kernel(
    tan_ref, tab_ref, lw_ref, cot_ref,
    back, fwd, recv, own, asend, arecv, bsend, brecv, zb, ysend,
    t_ssem, t_rsem, a_ssem, a_rsem, b_ssem, b_rsem, z_ssem, z_rsem, y_ssem, y_rsem,
):
    at = Place()

    def rows(pi):
        return pl.ds(pi * 2 * CAP, 2 * CAP)

    enter([at.q(q) for q in range(1, NQ)] + [at.dz(1), at.dz(-1)])
    for t in range(NK + 3):
        for k in range(NK):
            if 0 <= t - k < 4:
                pi = 3 - (t - k)
                for q in range(1, NQ):
                    send(
                        tan_ref.at[q, rows(pi), lanes(k)], recv.at[inverse(q), rows(pi), lanes(k)],
                        t_ssem, t_rsem.at[k, pi], at.q(q),
                    )
    for pi in (3, 2, 1, 0):
        both = slot_matrix(tab_ref, pi, True)
        fwd[pi] = both.astype(BF)
        back[pi] = both.T.astype(BF)

    def partial(k, pi):
        wait_bytes(recv.at[pl.ds(1, NQ - 1), rows(pi), lanes(k)], t_rsem.at[k, pi])
        arrived = jnp.concatenate(
            [tan_ref[0, rows(pi), lanes(k)]] + [recv[q, rows(pi), lanes(k)] for q in range(1, NQ)],
            axis=0,
        )
        return jnp.dot(back[pi], arrived, preferred_element_type=F32)

    def stage(k, n):
        d = sign(k)
        if n < 4:
            pi = 3 - n
            both = partial(k, pi)
            low, high = both[:TOK], both[TOK:]
            if n == 0:
                own[k] = low
                asend[k, 0] = high.astype(BF)
            else:
                s = 4 - n
                ahead, behind = (low, high) if d == 1 else (high, low)
                wait_bytes(arecv.at[k, n - 1], a_rsem.at[k, n - 1])
                asend[k, n] = (arecv[k, n - 1].astype(F32) + ahead).astype(BF)
                if n == 1:
                    bsend[k, 0] = behind.astype(BF)
                else:
                    wait_bytes(brecv.at[k, n - 2], b_rsem.at[k, n - 2])
                    bsend[k, n - 1] = (brecv[k, n - 2].astype(F32) + behind).astype(BF)
                send(bsend.at[k, n - 1], brecv.at[k, n - 1], b_ssem, b_rsem.at[k, n - 1], at.dz(-d))
            send(asend.at[k, n], arecv.at[k, n], a_ssem, a_rsem.at[k, n], at.dz(d))
            return
        if n == 4:
            wait_bytes(arecv.at[k, 3], a_rsem.at[k, 3])
            wait_bytes(brecv.at[k, 2], b_rsem.at[k, 2])
            combined = own[k] + arecv[k, 3].astype(F32) + brecv[k, 2].astype(F32)
            zb[k, 0] = (combined * lw_ref[...]).astype(BF)
            for t in (d, -d):
                send(zb.at[k, 0], zb.at[k, rel(-t)], z_ssem, z_rsem.at[k, rel(-t)], at.dz(t))
            return
        s = n - 4
        pi = s - 1
        wait_bytes(zb.at[k, rel(-d * s)], z_rsem.at[k, rel(-d * s)])
        if s < 4:
            wait_bytes(zb.at[k, rel(d * s)], z_rsem.at[k, rel(d * s)])
            send(
                zb.at[k, rel(-d * s)], zb.at[k, rel(-d * (s + 1))],
                z_ssem, z_rsem.at[k, rel(-d * (s + 1))], at.dz(d),
            )
        if s < 3:
            send(
                zb.at[k, rel(d * s)], zb.at[k, rel(d * (s + 1))],
                z_ssem, z_rsem.at[k, rel(d * (s + 1))], at.dz(-d),
            )
        r0, r1 = pair_blocks(pi)
        block = jnp.concatenate([zb[k, r0], zb[k, r1]], axis=0)
        picked = jnp.dot(fwd[pi], block, preferred_element_type=F32).astype(BF)
        cot_ref[0, rows(pi), lanes(k)] = picked[0 : 2 * CAP]
        for q in range(1, NQ):
            ysend[q, rows(pi), lanes(k)] = picked[q * 2 * CAP : (q + 1) * 2 * CAP]
        for q in range(1, NQ):
            send(
                ysend.at[q, rows(pi), lanes(k)], cot_ref.at[inverse(q), rows(pi), lanes(k)],
                y_ssem, y_rsem, at.q(q),
            )

    for t in range(NK + 8):
        for k in range(NK):
            if 0 <= t - k < 9:
                stage(k, t - k)

    wait_bytes(cot_ref.at[pl.ds(1, NQ - 1)], y_rsem)
    wait_bytes(tan_ref.at[pl.ds(1, NQ - 1)], t_ssem)
    wait_bytes(asend, a_ssem)
    wait_bytes(bsend, b_ssem)
    wait_bytes(zb.at[:, pl.ds(1, NZ - 1)], z_ssem)
    wait_bytes(cot_ref.at[pl.ds(1, NQ - 1)], y_ssem)


def sums_kernel(
    cv_ref, dir_ref, res_ref, damp_ref, out_ref, sum_ref,
    first, second, mine, group, c_ssem, c_rsem, a_ssem, a_rsem, b_ssem, b_rsem,
):
    at = Place()
    depth = cv_ref.shape[2]
    ff = cv_ref.shape[1]
    step = 16
    near = [(dz, dc) for dz in range(NZ) for dc in range(NC)][1:]
    wide = [(dy, dx) for dy in range(NY) for dx in range(NX)][1:]
    zc = [(at.expert(0, dz, dc), at.x) for dz, dc in near]
    yx = [(at.expert(dy, 0, 0), at.xi(dx)) for dy, dx in wide]
    enter(zc + yx)
    for d in (2, 1, 3):
        send(cv_ref.at[at.xi(d)], out_ref.at[at.x], c_ssem, c_rsem.at[NX - d], at.dx(d))
    scale = 1.0 / damp_ref[0]
    totals = (jnp.zeros((8, 128), F32),) * 4
    for d in (0, 1, 3, 2):
        who = at.xi(d)
        if d:
            wait_bytes(out_ref.at[who], c_rsem.at[d])

        def part(i, sums, d=d, who=who):
            sub = pl.ds(pl.multiple_of(i * step, step), step)
            cols = pl.ds(pl.multiple_of(who * depth, depth), depth)
            if d:
                c = out_ref[who, sub, :]
            else:
                c = cv_ref[who, sub, :]
                out_ref[who, sub, :] = c
            p = dir_ref[sub, cols].astype(F32)
            r = res_ref[sub, cols].astype(F32)
            g = p + c.astype(F32) * scale

            def fold(v):
                v = v[0:8] + v[8:16]
                t = v[:, 0:128]
                for j in range(1, depth // 128):
                    t = t + v[:, j * 128 : (j + 1) * 128]
                return t

            return (
                sums[0] + fold(p * g), sums[1] + fold(r * r),
                sums[2] + fold(r * g), sums[3] + fold(g * g),
            )

        totals = lax.fori_loop(0, ff // step, part, totals)
    row = lax.broadcasted_iota(jnp.int32, (8, 128), 0)
    tile = jnp.zeros((8, 128), F32)
    for i in range(4):
        tile = jnp.where(row == i, jnp.sum(totals[i]), tile)
    mine[...] = tile
    spot = at.z * NC + at.c
    first[spot] = tile
    for n, peer in enumerate(zc):
        send(mine, first.at[spot], a_ssem, a_rsem, peer)
    wait_bytes(first.at[pl.ds(0, 15)], a_rsem)
    tile = first[0]
    for i in range(1, NZ * NC):
        tile = tile + first[i]
    group[...] = tile
    spot = at.y * NX + at.x
    second[spot] = tile
    for n, peer in enumerate(yx):
        send(group, second.at[spot], b_ssem, b_rsem, peer)
    wait_bytes(second.at[pl.ds(0, 15)], b_rsem)
    tile = second[0]
    for i in range(1, NY * NX):
        tile = tile + second[i]
    sum_ref[...] = tile
    wait_bytes(first.at[pl.ds(0, 15)], a_ssem)
    wait_bytes(second.at[pl.ds(0, 15)], b_ssem)
    wait_bytes(out_ref.at[pl.ds(0, 3)], c_ssem)


def final_kernel(damp_ref, sum_ref, cv_ref, dir_ref, res_ref, step_ref, newr_ref, newd_ref):
    scale = 1.0 / damp_ref[0]
    pq, rr = sum_ref[0:1, 0:1], sum_ref[1:2, 0:1]
    rq, qq = sum_ref[2:3, 0:1], sum_ref[3:4, 0:1]
    alpha = rr / pq
    beta = (rr - 2.0 * alpha * rq + alpha * alpha * qq) / rr
    p = dir_ref[...].astype(F32)
    g = p + cv_ref[0].astype(F32) * scale
    updated = res_ref[...].astype(F32) - alpha * g
    step_ref[...] = (alpha * p).astype(BF)
    newr_ref[...] = updated.astype(BF)
    newd_ref[...] = (updated + beta * p).astype(BF)


def params(ident):
    return pltpu.CompilerParams(collective_id=ident, has_side_effects=True)


def per_device(
    tokens, routes, route_gates, loss_weights, damping, w_gate, w_up, direction, residual
):
    dma = pltpu.SemaphoreType.DMA
    depth = tokens.shape[1]
    ff_loc, width = direction.shape[1:]
    ff = ff_loc * NX
    per_q = NZ * CAP
    search, resid = direction[0], residual[0]
    shape = jax.ShapeDtypeStruct

    arrived, weights, search_cols, table = pl.pallas_call(
        tokens_kernel,
        out_shape=(
            shape((NQ, per_q, depth), BF), shape((depth, 2 * ff), BF),
            shape((NX, ff_loc, depth), BF), shape((NZ, 2 * NQ, TOK), F32),
        ),
        in_specs=[VMEM, VMEM, VMEM, ANY, ANY, ANY],
        out_specs=(VMEM, VMEM, VMEM, VMEM),
        scratch_shapes=[
            pltpu.VMEM((NZ, 2 * NQ, TOK), F32), pltpu.VMEM((4, NQ * 2 * CAP, 2 * TOK), BF),
            pltpu.VMEM((NK, NZ, TOK, CH), BF), pltpu.VMEM((NQ, per_q, depth), BF),
            pltpu.VMEM((width, ff_loc), BF), pltpu.VMEM((width, ff_loc), BF),
            pltpu.VMEM((NX, depth, 2 * ff_loc), BF), pltpu.VMEM((NX, depth, 2 * ff_loc), BF),
            dma, dma((NZ,)), dma, dma((NK, NZ)), dma, dma, dma, dma, dma, dma, dma((3,)),
        ],
        compiler_params=params(0),
        name="tokens_kernel",
    )(routes.T, route_gates.T, tokens, w_gate[0], w_up[0], search)

    products = jnp.dot(
        arrived.reshape(NQ * per_q, depth), weights, preferred_element_type=F32
    ).astype(BF)
    group = NQ * per_q // NX
    subs = 4
    small = (subs, group // subs, 2 * ff)
    hidden = pl.pallas_call(
        hidden_kernel,
        out_shape=shape((NX, group, ff), BF),
        in_specs=[VMEM],
        out_specs=VMEM,
        scratch_shapes=[pltpu.VMEM(small, BF)] * 4
        + [dma, dma((subs,)), dma, dma((subs,)), dma, dma((subs,)), dma, dma((subs, 3))],
        compiler_params=params(1),
        name="hidden_kernel",
    )(products.reshape(NX, group, 2 * ff))
    hidden = hidden.reshape(NQ * per_q, ff)
    tangent = jnp.dot(
        hidden, search_cols.reshape(ff, depth), preferred_element_type=F32
    ).astype(BF)
    block = (TOK, CH)
    cotangent = pl.pallas_call(
        cotangent_kernel,
        out_shape=shape((NQ, per_q, depth), BF),
        in_specs=[VMEM, VMEM, VMEM],
        out_specs=VMEM,
        scratch_shapes=[
            pltpu.VMEM((4, 2 * TOK, NQ * 2 * CAP), BF), pltpu.VMEM((4, NQ * 2 * CAP, 2 * TOK), BF),
            pltpu.VMEM((NQ, per_q, depth), BF), pltpu.VMEM((NK,) + block, F32),
            pltpu.VMEM((NK, 4) + block, BF), pltpu.VMEM((NK, 4) + block, BF),
            pltpu.VMEM((NK, 3) + block, BF), pltpu.VMEM((NK, 3) + block, BF),
            pltpu.VMEM((NK, NZ) + block, BF), pltpu.VMEM((NQ, per_q, depth), BF),
            dma, dma((NK, 4)), dma, dma((NK, 4)), dma, dma((NK, 3)), dma, dma((NK, NZ)), dma, dma,
        ],
        compiler_params=params(2),
        name="cotangent_kernel",
    )(tangent.reshape(NQ, per_q, depth), table, loss_weights[:, None])
    curvature = lax.dot_general(
        hidden, cotangent.reshape(NQ * per_q, depth), (((0,), (0,)), ((), ())),
        preferred_element_type=F32,
    ).astype(BF)
    smem = pl.BlockSpec(memory_space=pltpu.SMEM)
    tile = (8, 128)
    mine, sums = pl.pallas_call(
        sums_kernel,
        out_shape=(shape((NX, ff_loc, depth), BF), shape(tile, F32)),
        in_specs=[VMEM, VMEM, VMEM, smem],
        out_specs=(VMEM, VMEM),
        scratch_shapes=[
            pltpu.VMEM((16,) + tile, F32), pltpu.VMEM((16,) + tile, F32),
            pltpu.VMEM(tile, F32), pltpu.VMEM(tile, F32),
            dma, dma((NX,)), dma, dma, dma, dma,
        ],
        compiler_params=params(3),
        name="sums_kernel",
    )(curvature.reshape(NX, ff_loc, depth), search, resid, damping)
    flat = pl.BlockSpec((ff_loc, depth), lambda i: (0, i))
    outs = pl.pallas_call(
        final_kernel,
        out_shape=(shape((ff_loc, width), BF),) * 3,
        grid=(NX,),
        in_specs=[
            smem, pl.BlockSpec(tile, lambda i: (0, 0)),
            pl.BlockSpec((1, ff_loc, depth), lambda i: (i, 0, 0)), flat, flat,
        ],
        out_specs=(flat, flat, flat),
        name="final_kernel",
    )(damping, sums, mine, search, resid)
    return tuple(o[None] for o in outs)


def solution(mesh):
    return jax.shard_map(
        per_device,
        mesh=mesh,
        in_specs=(
            P("expert", "hidden"),
            P("expert", None),
            P("expert", None),
            P("expert"),
            P(),
            P("expert", None, "hidden"),
            P("expert", None, "hidden"),
            P("expert", "hidden", None),
            P("expert", "hidden", None),
        ),
        out_specs=(
            P("expert", "hidden", None),
            P("expert", "hidden", None),
            P("expert", "hidden", None),
        ),
        check_vma=False,
    )
```

```python
import jax
import jax.numpy as jnp
from jax import lax
from jax.experimental import pallas as pl
from jax.experimental.pallas import tpu as pltpu
from jax.sharding import PartitionSpec as P

MESH = pl.DeviceIdType.MESH
BF = jnp.bfloat16
F32 = jnp.float32
NY, NZ, NC, NX = 4, 8, 2, 4
NQ = NY * NC
CAP = 24
TOK = 128
CH = 256
NK = 4
VMEM = pl.BlockSpec(memory_space=pltpu.VMEM)
ANY = pl.BlockSpec(memory_space=pl.ANY)


class Place:
    def __init__(self):
        self.e = lax.axis_index("expert")
        self.x = lax.axis_index("hidden")
        self.y = self.e // (NZ * NC)
        self.z = (self.e // NC) % NZ
        self.c = self.e % NC

    def expert(self, dy, dz, dc):
        return (
            ((self.y + dy) % NY) * (NZ * NC)
            + ((self.z + dz) % NZ) * NC
            + (self.c + dc) % NC
        )

    def q(self, q):
        return (self.expert(q // NC, 0, q % NC), self.x)

    def dz(self, d):
        return (self.expert(0, d, 0), self.x)

    def offset(self, dy, dz, dc, dx):
        return (self.expert(dy, dz, dc), self.xi(dx))

    def dx(self, d):
        return (self.e, self.xi(d))

    def xi(self, d):
        return (self.x + d) % NX


def inverse(q):
    return ((NY - q // NC) % NY) * NC + q % NC


def enter(peers):
    barrier = pltpu.get_barrier_semaphore()
    for peer in peers:
        pl.semaphore_signal(barrier, inc=1, device_id=peer, device_id_type=MESH)
    pl.semaphore_wait(barrier, len(peers))


def send(src, dst, ssem, rsem, peer):
    pltpu.make_async_remote_copy(
        src_ref=src, dst_ref=dst, send_sem=ssem, recv_sem=rsem, device_id=peer, device_id_type=MESH
    ).start()


def wait_bytes(ref, sem):
    pltpu.make_async_copy(ref, ref, sem).wait()


def pair_blocks(pi):
    return (0, 4) if pi == 3 else (pi + 1, NZ - 1 - pi)


def slot_matrix(tab_ref, pi, weighted):
    r0, r1 = pair_blocks(pi)
    slot = lax.broadcasted_iota(jnp.int32, (CAP, TOK), 0).astype(F32)
    zero = jnp.zeros((CAP, TOK), F32)
    rows = []
    for q in range(NQ):
        parts = []
        for r in (r0, r1):
            hit = tab_ref[r, q : q + 1, :] == slot
            value = tab_ref[r, NQ + q : NQ + q + 1, :] if weighted else jnp.ones((1, TOK), F32)
            parts.append(jnp.where(hit, value, 0.0))
        rows.append(jnp.concatenate([parts[0], zero], axis=1))
        rows.append(jnp.concatenate([zero, parts[1]], axis=1))
    return jnp.concatenate(rows, axis=0)


def lanes(k):
    return pl.ds(k * CH, CH)


def sign(k):
    return 1 if k % 2 == 0 else -1


def rel(r):
    return r % NZ


def tokens_kernel(
    routes_ref, gates_ref, tok_ref, wg_ref, wu_ref, dir_ref,
    x_ref, w_ref, dirc_ref, tab_ref,
    own_tab, slots, zb, ysend,
    tab_ssem, tab_rsem, z_ssem, z_rsem, y_ssem, y_rsem, d_ssem, d_rsem, w_ssem, w_rsem, loc,
):
    at = Place()
    depth = dir_ref.shape[1] // NX

    def block(d, width=depth):
        return pl.ds(pl.multiple_of(at.xi(d) * depth, depth), width)

    own = [
        pltpu.make_async_copy(wg_ref.at[:, block(0)], w_ref.at[0, at.x], loc.at[0]),
        pltpu.make_async_copy(wu_ref.at[:, block(0)], w_ref.at[1, at.x], loc.at[1]),
        pltpu.make_async_copy(dir_ref.at[:, block(0, CH)], dirc_ref.at[at.x], loc.at[2]),
    ]
    for copy in own:
        copy.start()

    row = lax.broadcasted_iota(jnp.int32, (NZ * NQ, TOK), 0)
    ids = (
        ((at.y + ((row >> 1) & 3)) & (NY - 1)) * (NZ * NC)
        + ((at.z + (row >> 3)) & (NZ - 1)) * NC
        + ((at.c + row) & 1)
    )
    named = jnp.zeros((NZ * NQ, TOK), F32)
    gate = jnp.zeros((NZ * NQ, TOK), F32)
    for j in range(routes_ref.shape[0]):
        same = routes_ref[j : j + 1, :] == ids
        named = named + jnp.where(same, 1.0, 0.0)
        gate = gate + jnp.where(same, gates_ref[j : j + 1, :], 0.0)
    before = (
        lax.broadcasted_iota(jnp.int32, (TOK, TOK), 0) < lax.broadcasted_iota(jnp.int32, (TOK, TOK), 1)
    )
    place = jnp.dot(
        named.astype(BF), jnp.where(before, 1.0, 0.0).astype(BF), preferred_element_type=F32
    )
    place = jnp.where(named > 0.0, place, -1.0)
    for r in range(NZ):
        own_tab[r, 0:NQ, :] = place[r * NQ : (r + 1) * NQ]
        own_tab[r, NQ : 2 * NQ, :] = gate[r * NQ : (r + 1) * NQ]
    tab_ref[0] = own_tab[0]

    enter(
        [at.q(q) for q in range(1, NQ)] + [at.dz(d) for d in range(1, NZ)] + [at.dx(d) for d in range(1, NX)]
    )
    for r in (1, 7, 2, 6, 3, 5, 4):
        send(own_tab.at[r], tab_ref.at[rel(-r)], tab_ssem, tab_rsem.at[rel(-r)], at.dz(r))
    for k in range(NK):
        for d in (1, -1):
            send(
                tok_ref.at[:, lanes(k)], zb.at[k, rel(-d)], z_ssem, z_rsem.at[k, rel(-d)], at.dz(d)
            )
    for d in (2, 1, 3):
        send(wg_ref.at[:, block(d)], w_ref.at[0, at.x], w_ssem, w_rsem, at.dx(d))
        send(wu_ref.at[:, block(d)], w_ref.at[1, at.x], w_ssem, w_rsem, at.dx(d))
    for d in (2, 1, 3):
        send(dir_ref.at[:, block(d, CH)], dirc_ref.at[at.x], d_ssem, d_rsem, at.dx(d))

    for s in range(1, 5):
        pi = s - 1
        for r in pair_blocks(pi):
            if r:
                wait_bytes(tab_ref.at[r], tab_rsem.at[r])
        slots[pi] = slot_matrix(tab_ref, pi, False).astype(BF)
        for k in range(NK):
            d = sign(k)
            wait_bytes(zb.at[k, rel(-d * s)], z_rsem.at[k, rel(-d * s)])
            if s < 4:
                wait_bytes(zb.at[k, rel(d * s)], z_rsem.at[k, rel(d * s)])
                send(
                    zb.at[k, rel(-d * s)], zb.at[k, rel(-d * (s + 1))],
                    z_ssem, z_rsem.at[k, rel(-d * (s + 1))], at.dz(d),
                )
            if s < 3:
                send(
                    zb.at[k, rel(d * s)], zb.at[k, rel(d * (s + 1))],
                    z_ssem, z_rsem.at[k, rel(d * (s + 1))], at.dz(-d),
                )
            r0, r1 = pair_blocks(pi)
            first = tok_ref[:, lanes(k)] if r0 == 0 else zb[k, r0]
            both = jnp.concatenate([first, zb[k, r1]], axis=0)
            picked = jnp.dot(slots[pi], both, preferred_element_type=F32).astype(BF)
            rows = pl.ds(pi * 2 * CAP, 2 * CAP)
            x_ref[0, rows, lanes(k)] = picked[0 : 2 * CAP]
            for q in range(1, NQ):
                ysend[q, rows, lanes(k)] = picked[q * 2 * CAP : (q + 1) * 2 * CAP]
            for q in range(1, NQ):
                send(
                    ysend.at[q, rows, lanes(k)], x_ref.at[inverse(q), rows, lanes(k)],
                    y_ssem, y_rsem, at.q(q),
                )

    for copy in own:
        copy.wait()
    for sem in (w_rsem, w_ssem):
        wait_bytes(w_ref.at[:, pl.ds(1, 3)], sem)
    for sem in (d_rsem, d_ssem):
        wait_bytes(dirc_ref.at[pl.ds(1, 3)], sem)
    for sem in (y_rsem, y_ssem):
        wait_bytes(x_ref.at[pl.ds(1, NQ - 1)], sem)
    wait_bytes(own_tab.at[pl.ds(1, NZ - 1)], tab_ssem)
    wait_bytes(zb.at[:, pl.ds(1, NZ - 1)], z_ssem)


def hidden_kernel(
    p_ref, h_ref, far, acc, accin, near,
    f_ssem, f_rsem, a_ssem, a_rsem, n_ssem, n_rsem, h_ssem, h_rsem,
):
    at = Place()
    subs = far.shape[0]
    rows_of = far.shape[1]
    ff = h_ref.shape[2]
    step = 16
    enter([at.dx(1), at.dx(-1)])

    def rows(u):
        return pl.ds(u * rows_of, rows_of)

    for u in range(subs):
        d = sign(u)
        send(p_ref.at[at.xi(2), rows(u)], far.at[u], f_ssem, f_rsem.at[u], at.dx(-d))
        send(p_ref.at[at.xi(d), rows(u)], near.at[u], n_ssem, n_rsem.at[u], at.dx(d))
    for u in range(subs):
        d = sign(u)
        wait_bytes(far.at[u], f_rsem.at[u])

        def add(i, _, u=u, d=d):
            sub = pl.ds(pl.multiple_of(i * step, step), step)
            mine = p_ref[at.xi(-d), pl.ds(pl.multiple_of(u * rows_of + i * step, step), step), :]
            acc[u, sub, :] = (far[u, sub, :].astype(F32) + mine.astype(F32)).astype(BF)
            return 0

        lax.fori_loop(0, rows_of // step, add, 0)
        send(acc.at[u], accin.at[u], a_ssem, a_rsem.at[u], at.dx(-d))
    for u in range(subs):
        d = sign(u)
        wait_bytes(near.at[u], n_rsem.at[u])
        wait_bytes(accin.at[u], a_rsem.at[u])

        def act(i, _, u=u):
            sub = pl.ds(pl.multiple_of(i * step, step), step)
            whole = pl.ds(pl.multiple_of(u * rows_of + i * step, step), step)

            def total(cols):
                return (
                    p_ref[at.x, whole, cols].astype(F32)
                    + accin[u, sub, cols].astype(F32)
                    + near[u, sub, cols].astype(F32)
                )

            v = total(pl.ds(0, ff))
            h_ref[at.x, whole, :] = (v / (1.0 + jnp.exp(-v)) * total(pl.ds(ff, ff))).astype(BF)
            return 0

        lax.fori_loop(0, rows_of // step, act, 0)
        for t in (d, -d):
            send(
                h_ref.at[at.x, rows(u)], h_ref.at[at.x, rows(u)],
                h_ssem, h_rsem.at[u, 0 if t == d else 1], at.dx(t),
            )
    for u in range(subs):
        d = sign(u)
        wait_bytes(h_ref.at[at.xi(-d), rows(u)], h_rsem.at[u, 0])
        send(
            h_ref.at[at.xi(-d), rows(u)], h_ref.at[at.xi(-d), rows(u)],
            h_ssem, h_rsem.at[u, 2], at.dx(d),
        )
    for u in range(subs):
        d = sign(u)
        wait_bytes(h_ref.at[at.xi(d), rows(u)], h_rsem.at[u, 1])
        wait_bytes(h_ref.at[at.xi(2), rows(u)], h_rsem.at[u, 2])
    wait_bytes(far, f_ssem)
    wait_bytes(near, n_ssem)
    wait_bytes(acc, a_ssem)
    wait_bytes(h_ref.at[pl.ds(0, 3)], h_ssem)


GAP = 3


def curvature_kernel(
    damp_ref, hid_ref, first_ref, tab_ref, lw_ref, dir_ref, res_ref, out_ref, sum_ref,
    back, fwd, turned, dcols, tsend, recv, own, asend, arecv, bsend, brecv, zb, ysend, cot, csend,
    gather1, gather2, mine, group,
    d_ssem, d_rsem, t_ssem, t_rsem, a_ssem, a_rsem, b_ssem, b_rsem, z_ssem, z_rsem,
    y_ssem, y_rsem, c_ssem, c_rsem, r_ssem, r_rsem, s_ssem, s_rsem,
):
    at = Place()
    ff, depth = dcols.shape[1] * NX, dcols.shape[2]
    ff_loc = dcols.shape[1]
    per_q = NZ * CAP
    near = [(0, dz, dc, 0) for dz in range(NZ) for dc in range(NC)][1:]
    wide = [(dy, 0, 0, dx) for dy in range(NY) for dx in range(NX)][1:]
    diag = [(dy, 0, 1, 0) for dy in range(1, NY)]
    enter([at.offset(*o) for o in near + wide + diag])

    def rows(q, pi):
        return pl.ds(q * per_q + pi * 2 * CAP, 2 * CAP)

    rest = pl.ds(per_q, (NQ - 1) * per_q)

    for k in range(1, NK):
        for d in (2, 1, 3):
            cols = pl.ds(pl.multiple_of(at.xi(d) * depth + k * CH, CH), CH)
            send(
                dir_ref.at[:, cols], dcols.at[at.x, :, lanes(k)], d_ssem, d_rsem.at[k], at.dx(d)
            )

    def tangent(k):
        if k:
            cols = pl.ds(pl.multiple_of(at.x * depth + k * CH, CH), CH)
            dcols[at.x, :, lanes(k)] = dir_ref[:, cols]
            wait_bytes(dcols.at[pl.ds(1, 3), :, lanes(k)], d_rsem.at[k])
            search = dcols[:, :, lanes(k)].reshape(ff, CH)
        else:
            search = first_ref[...].reshape(ff, CH)
        tsend[:, lanes(k)] = jnp.dot(
            hid_ref[...], search, preferred_element_type=F32
        ).astype(BF)
        for pi in (3, 2, 1, 0):
            for q in range(1, NQ):
                send(
                    tsend.at[rows(q, pi), lanes(k)], recv.at[rows(inverse(q), pi), lanes(k)],
                    t_ssem, t_rsem.at[k, pi], at.q(q),
                )

    def partial(k, pi):
        wait_bytes(recv.at[pl.ds(0, (NQ - 1) * 2 * CAP), lanes(k)], t_rsem.at[k, pi])
        arrived = jnp.concatenate(
            [tsend[rows(0, pi), lanes(k)]] + [recv[rows(q, pi), lanes(k)] for q in range(1, NQ)],
            axis=0,
        )
        return jnp.dot(back[pi], arrived, preferred_element_type=F32)

    def stage(k, n):
        d = sign(k)
        if n < 4:
            pi = 3 - n
            both = partial(k, pi)
            low, high = both[:TOK], both[TOK:]
            if n == 0:
                own[k] = low
                asend[k, 0] = high.astype(BF)
            else:
                ahead, behind = (low, high) if d == 1 else (high, low)
                wait_bytes(arecv.at[k, n - 1], a_rsem.at[k, n - 1])
                asend[k, n] = (arecv[k, n - 1].astype(F32) + ahead).astype(BF)
                if n == 1:
                    bsend[k, 0] = behind.astype(BF)
                else:
                    wait_bytes(brecv.at[k, n - 2], b_rsem.at[k, n - 2])
                    bsend[k, n - 1] = (brecv[k, n - 2].astype(F32) + behind).astype(BF)
                send(bsend.at[k, n - 1], brecv.at[k, n - 1], b_ssem, b_rsem.at[k, n - 1], at.dz(-d))
            send(asend.at[k, n], arecv.at[k, n], a_ssem, a_rsem.at[k, n], at.dz(d))
            return
        if n == 4:
            wait_bytes(arecv.at[k, 3], a_rsem.at[k, 3])
            wait_bytes(brecv.at[k, 2], b_rsem.at[k, 2])
            combined = own[k] + arecv[k, 3].astype(F32) + brecv[k, 2].astype(F32)
            zb[k, 0] = (combined * lw_ref[...]).astype(BF)
            for t in (d, -d):
                send(zb.at[k, 0], zb.at[k, rel(-t)], z_ssem, z_rsem.at[k, rel(-t)], at.dz(t))
            return
        s = n - 4
        pi = s - 1
        wait_bytes(zb.at[k, rel(-d * s)], z_rsem.at[k, rel(-d * s)])
        if s < 4:
            wait_bytes(zb.at[k, rel(d * s)], z_rsem.at[k, rel(d * s)])
            send(
                zb.at[k, rel(-d * s)], zb.at[k, rel(-d * (s + 1))],
                z_ssem, z_rsem.at[k, rel(-d * (s + 1))], at.dz(d),
            )
        if s < 3:
            send(
                zb.at[k, rel(d * s)], zb.at[k, rel(d * (s + 1))],
                z_ssem, z_rsem.at[k, rel(d * (s + 1))], at.dz(-d),
            )
        r0, r1 = pair_blocks(pi)
        both = jnp.concatenate([zb[k, r0], zb[k, r1]], axis=0)
        picked = jnp.dot(fwd[pi], both, preferred_element_type=F32).astype(BF)
        cot[rows(0, pi), lanes(k)] = picked[0 : 2 * CAP]
        for q in range(1, NQ):
            ysend[rows(q, pi), lanes(k)] = picked[q * 2 * CAP : (q + 1) * 2 * CAP]
        for q in range(1, NQ):
            send(
                ysend.at[rows(q, pi), lanes(k)], cot.at[rows(inverse(q), pi), lanes(k)],
                y_ssem, y_rsem.at[k], at.q(q),
            )

    def turn():
        turned[...] = hid_ref[...].T

    def matrices():
        for pi in (3, 2, 1, 0):
            both = slot_matrix(tab_ref, pi, True)
            fwd[pi] = both.astype(BF)
            back[pi] = both.T.astype(BF)

    def curvature(k):
        wait_bytes(cot.at[rest, lanes(k)], y_rsem.at[k])
        csend[k] = jnp.dot(
            turned[...], cot[:, lanes(k)], preferred_element_type=F32
        ).astype(BF).reshape(NX, ff_loc, CH)
        for d in (2, 1, 3):
            send(csend.at[k, at.xi(d)], out_ref.at[at.x, :, lanes(k)], c_ssem, c_rsem.at[k], at.dx(d))
        out_ref[at.x, :, lanes(k)] = csend[k, at.x]

    scale = 1.0 / damp_ref[0]
    step = 16

    def total(k, sums):
        wait_bytes(out_ref.at[pl.ds(1, 3), :, lanes(k)], c_rsem.at[k])

        def part(i, sums):
            sub = pl.ds(pl.multiple_of(i * step, step), step)
            for j in range(NX):
                cols = pl.ds(j * depth + k * CH, CH)
                p = dir_ref[sub, cols].astype(F32)
                r = res_ref[sub, cols].astype(F32)
                g = p + out_ref[j, sub, lanes(k)].astype(F32) * scale

                def fold(v):
                    v = v[0:8] + v[8:16]
                    return v[:, 0:128] + v[:, 128:256]

                sums = (
                    sums[0] + fold(p * g), sums[1] + fold(r * r),
                    sums[2] + fold(r * g), sums[3] + fold(g * g),
                )
            return sums

        return lax.fori_loop(0, ff_loc // step, part, sums)

    tangent(0)
    matrices()
    events = [(GAP * k + n, 1, k, n) for k in range(NK) for n in range(9)]
    events += [(GAP * k - 2, 0, k, 0) for k in range(1, NK)] + [(4, 2, 0, 0)]
    for _, kind, k, n in sorted(events):
        if kind == 0:
            tangent(k)
        elif kind == 1:
            stage(k, n)
        else:
            turn()
    for k in range(NK):
        curvature(k)
    sums = (jnp.zeros((8, 128), F32),) * 4
    for k in range(NK):
        sums = total(k, sums)

    row = lax.broadcasted_iota(jnp.int32, (8, 128), 0)
    tile = jnp.zeros((8, 128), F32)
    for i in range(4):
        tile = jnp.where(row == i, jnp.sum(sums[i]), tile)
    mine[...] = tile
    spot = at.z * NC + at.c
    gather1[spot] = tile
    for o in near:
        send(mine, gather1.at[spot], r_ssem, r_rsem, at.offset(*o))
    wait_bytes(gather1.at[pl.ds(0, 15)], r_rsem)
    tile = gather1[0]
    for i in range(1, NZ * NC):
        tile = tile + gather1[i]
    group[...] = tile
    spot = at.y * NX + at.x
    gather2[spot] = tile
    for o in wide:
        send(group, gather2.at[spot], s_ssem, s_rsem, at.offset(*o))
    wait_bytes(gather2.at[pl.ds(0, 15)], s_rsem)
    tile = gather2[0]
    for i in range(1, NY * NX):
        tile = tile + gather2[i]
    sum_ref[...] = tile

    wait_bytes(dcols.at[pl.ds(1, 3), :, pl.ds(CH, (NK - 1) * CH)], d_ssem)
    wait_bytes(tsend.at[rest], t_ssem)
    wait_bytes(asend, a_ssem)
    wait_bytes(bsend, b_ssem)
    wait_bytes(zb.at[:, pl.ds(1, NZ - 1)], z_ssem)
    wait_bytes(cot.at[rest], y_ssem)
    wait_bytes(csend.at[:, pl.ds(1, 3)], c_ssem)
    wait_bytes(gather1.at[pl.ds(0, 15)], r_ssem)
    wait_bytes(gather2.at[pl.ds(0, 15)], s_ssem)


def final_kernel(damp_ref, sum_ref, cv_ref, dir_ref, res_ref, step_ref, newr_ref, newd_ref):
    scale = 1.0 / damp_ref[0]
    pq, rr = sum_ref[0:1, 0:1], sum_ref[1:2, 0:1]
    rq, qq = sum_ref[2:3, 0:1], sum_ref[3:4, 0:1]
    alpha = rr / pq
    beta = (rr - 2.0 * alpha * rq + alpha * alpha * qq) / rr
    p = dir_ref[...].astype(F32)
    g = p + cv_ref[0].astype(F32) * scale
    updated = res_ref[...].astype(F32) - alpha * g
    step_ref[...] = (alpha * p).astype(BF)
    newr_ref[...] = updated.astype(BF)
    newd_ref[...] = (updated + beta * p).astype(BF)


def params(ident):
    return pltpu.CompilerParams(collective_id=ident, has_side_effects=True)


def per_device(
    tokens, routes, route_gates, loss_weights, damping, w_gate, w_up, direction, residual
):
    dma = pltpu.SemaphoreType.DMA
    depth = tokens.shape[1]
    ff_loc, width = direction.shape[1:]
    ff = ff_loc * NX
    per_q = NZ * CAP
    search, resid = direction[0], residual[0]
    shape = jax.ShapeDtypeStruct

    slots = NQ * per_q
    arrived, weights, first_cols, table = pl.pallas_call(
        tokens_kernel,
        out_shape=(
            shape((NQ, per_q, depth), BF), shape((2, NX, ff_loc, depth), BF),
            shape((NX, ff_loc, CH), BF), shape((NZ, 2 * NQ, TOK), F32),
        ),
        in_specs=[VMEM, VMEM, VMEM, ANY, ANY, ANY],
        out_specs=(VMEM, VMEM, VMEM, VMEM),
        scratch_shapes=[
            pltpu.VMEM((NZ, 2 * NQ, TOK), F32), pltpu.VMEM((4, NQ * 2 * CAP, 2 * TOK), BF),
            pltpu.VMEM((NK, NZ, TOK, CH), BF), pltpu.VMEM((NQ, per_q, depth), BF),
            dma, dma((NZ,)), dma, dma((NK, NZ)), dma, dma, dma, dma, dma, dma, dma((3,)),
        ],
        compiler_params=params(0),
        name="tokens_kernel",
    )(routes.T, route_gates.T, tokens, w_gate[0].T, w_up[0].T, search)

    products = lax.dot_general(
        arrived.reshape(slots, depth), weights.reshape(2 * ff, depth), (((1,), (1,)), ((), ())),
        preferred_element_type=F32,
    ).astype(BF)
    group = slots // NX
    subs = 4
    small = (subs, group // subs, 2 * ff)
    hidden = pl.pallas_call(
        hidden_kernel,
        out_shape=shape((NX, group, ff), BF),
        in_specs=[VMEM],
        out_specs=VMEM,
        scratch_shapes=[pltpu.VMEM(small, BF)] * 4
        + [dma, dma((subs,)), dma, dma((subs,)), dma, dma((subs,)), dma, dma((subs, 3))],
        compiler_params=params(1),
        name="hidden_kernel",
    )(products.reshape(NX, group, 2 * ff))
    block = (TOK, CH)
    tile = (8, 128)
    smem = pl.BlockSpec(memory_space=pltpu.SMEM)
    vmem = pltpu.VMEM
    mine, sums = pl.pallas_call(
        curvature_kernel,
        out_shape=(shape((NX, ff_loc, depth), BF), shape(tile, F32)),
        in_specs=[smem] + [VMEM] * 6,
        out_specs=(VMEM, VMEM),
        scratch_shapes=[
            vmem((4, 2 * TOK, NQ * 2 * CAP), BF), vmem((4, NQ * 2 * CAP, 2 * TOK), BF),
            vmem((ff, slots), BF), vmem((NX, ff_loc, depth), BF),
            vmem((slots, depth), BF), vmem((slots, depth), BF), vmem((NK,) + block, F32),
            vmem((NK, 4) + block, BF), vmem((NK, 4) + block, BF),
            vmem((NK, 3) + block, BF), vmem((NK, 3) + block, BF),
            vmem((NK, NZ) + block, BF), vmem((slots, depth), BF), vmem((slots, depth), BF),
            vmem((NK, NX, ff_loc, CH), BF),
            vmem((16,) + tile, F32), vmem((16,) + tile, F32), vmem(tile, F32), vmem(tile, F32),
            dma, dma((NK,)), dma, dma((NK, 4)), dma, dma((NK, 4)), dma, dma((NK, 3)),
            dma, dma((NK, NZ)), dma, dma((NK,)), dma, dma((NK,)), dma, dma, dma, dma,
        ],
        compiler_params=params(2),
        name="curvature_kernel",
    )(damping, hidden.reshape(slots, ff), first_cols, table, loss_weights[:, None], search, resid)
    flat = pl.BlockSpec((ff_loc, depth), lambda i: (0, i))
    outs = pl.pallas_call(
        final_kernel,
        out_shape=(shape((ff_loc, width), BF),) * 3,
        grid=(NX,),
        in_specs=[
            smem, pl.BlockSpec(tile, lambda i: (0, 0)),
            pl.BlockSpec((1, ff_loc, depth), lambda i: (i, 0, 0)), flat, flat,
        ],
        out_specs=(flat, flat, flat),
        name="final_kernel",
    )(damping, sums, mine, search, resid)
    return tuple(o[None] for o in outs)


def solution(mesh):
    return jax.shard_map(
        per_device,
        mesh=mesh,
        in_specs=(
            P("expert", "hidden"),
            P("expert", None),
            P("expert", None),
            P("expert"),
            P(),
            P("expert", None, "hidden"),
            P("expert", None, "hidden"),
            P("expert", "hidden", None),
            P("expert", "hidden", None),
        ),
        out_specs=(
            P("expert", "hidden", None),
            P("expert", "hidden", None),
            P("expert", "hidden", None),
        ),
        check_vma=False,
    )
```
